32 devices in a mesh: seq: 8 (over y, x, core), mp: 4 (over z).
Axes of the slice: x: 2, y: 2, z: 4, core: 2. Of those that a mesh axis runs over, the one named last changes fastest.
Arguments:
- queries: bfloat16 [8, 96, 64, 128], P('seq', None, 'mp'), may hold values from -12 to 12
- new_keys: bfloat16 [8, 96, 8, 128], P('seq', None, 'mp'), may hold values from -8 to 8
- new_values: bfloat16 [8, 96, 8, 128], P('seq', None, 'mp'), may hold values from -6 to 6
- pool_keys: bfloat16 [128, 8, 128, 128], P('seq', 'mp'), may hold values from -8 to 8
- pool_values: bfloat16 [128, 8, 128, 128], P('seq', 'mp'), may hold values from -6 to 6
- prefix_len: int32 [8], replicated, may hold values from 1 to 2048, as said below
- page_table: int32 [8, 16], replicated, may hold values from -1 to 127, as said below
- out_weight: bfloat16 [8192, 8192], P('mp'), may hold values from -0.0625 to 0.0625
Outputs:
- attended: bfloat16 [8, 96, 8192], P('seq', None, 'mp')
The draws below stay inside these ranges and needn't reach their ends.
Inputs may be any that keep to these rules, and one draw needn't show every extreme that they name: Prompt r's prefix holds prefix_len[r] tokens in its first ceil(prefix_len[r] / 128) page-table entries. `page_table`: entry [r, l] is the pool page holding positions l * 128 to l * 128 + 127 of prompt r's prefix; entries past the prefix are -1; no pool page appears twice in the table. Pool page p lies on seq index p // 16; one row of the table names at most 2 pages of one seq index, and some row names exactly 2 pages of some seq index.
All inputs are finite; a program needn't handle non-finite values.
Results may differ from the reference program's by a relative error of at most 0.012.
Values may be sent and summed in bfloat16 or wider, within the bound.
A program may use at most 192 MiB of HBM per device.

```python
import jax
import jax.numpy as jnp
from jax import lax

D = 8192
QH = 64
KVH = 8
HD = 128
PAGE = 128
C = 96
R_DEV = 1
P_DEV = 16
REQS = 8
POOL = 128
MAXP = 16
N_SEQ = 8
N_MP = 4


def page_plan(key):
    key = jax.random.fold_in(key, 7)
    key_counts, key_long, key_tail, key_shift = jax.random.split(key, 4)
    hold_most = (MAXP + N_SEQ - 1) // N_SEQ
    others_most = min((POOL - MAXP) // (REQS - 1), MAXP - 1, N_SEQ, (P_DEV - hold_most) // R_DEV)
    counts = jax.random.randint(key_counts, (REQS,), 1, others_most + 1)
    longest = jax.random.randint(key_long, (), 0, REQS)
    is_long = jnp.arange(REQS) == longest
    counts = jnp.where(is_long, MAXP, counts)
    tail_tokens = jax.random.randint(key_tail, (REQS,), 1, PAGE + 1)
    lengths = jnp.where(is_long, MAXP * PAGE, (counts - 1) * PAGE + tail_tokens)
    slot_ids = jnp.arange(MAXP)
    homes = jnp.arange(REQS) // R_DEV
    stride = N_SEQ // 2 - 1
    device_ids = (homes[:, None] + N_SEQ // 2 + slot_ids[None, :] * stride) % N_SEQ
    valid = slot_ids[None, :] < counts[:, None]
    on_device = (device_ids[:, :, None] == jnp.arange(N_SEQ)[None, None, :]) & valid[:, :, None]
    flat = on_device.reshape(REQS * MAXP, N_SEQ).astype(jnp.int32)
    ranks = jnp.cumsum(flat, axis=0) - 1
    rank = jnp.sum(jnp.where(flat > 0, ranks, 0), axis=1).reshape(REQS, MAXP)
    shifts = jax.random.randint(key_shift, (N_SEQ,), 0, P_DEV)
    slots = (rank + shifts[device_ids]) % P_DEV
    table = jnp.where(valid, device_ids * P_DEV + slots, -1)
    return (lengths.astype(jnp.int32), table.astype(jnp.int32))


def draw_prefix_len(key, part):
    return page_plan(key)[0]


def draw_page_table(key, part):
    return page_plan(key)[1]


def attention_plan(key):
    key = jax.random.fold_in(key, 11)
    key_query, key_spread, key_keys = jax.random.split(key, 3)
    base = jax.random.normal(key_query, (REQS, C, QH, HD), jnp.float32)
    spread = jnp.exp(jax.random.uniform(key_spread, (REQS, C, QH, 1), jnp.float32, jnp.log(0.5), jnp.log(4.0)))
    query_draw = jnp.clip(base * spread, -12.0, 12.0)
    key_draw = jnp.clip(jax.random.normal(key_keys, (REQS, C, KVH, HD), jnp.float32), -8.0, 8.0)
    return (query_draw, key_draw)


def draw_queries(key, part):
    return attention_plan(key)[0].astype(jnp.bfloat16)


def draw_new_keys(key, part):
    return attention_plan(key)[1].astype(jnp.bfloat16)


def steps_of(rng, extent, cuts, smallest, top_value):
    gain, own = 1.0, jax.random.fold_in(rng, 6)
    for dim, parts in cuts:
        steps = jnp.exp(jax.random.uniform(jax.random.fold_in(own, dim), (parts,), jnp.float32, smallest / len(cuts), top_value / len(cuts)))
        gain = gain * jnp.repeat(steps, extent[dim] // parts).reshape([-1 if axis == dim else 1 for axis in range(len(extent))])
    return gain


def normal_values(rng, shape, scale, bound, cuts=(), kind=jnp.bfloat16):
    drawn = jax.random.normal(rng, shape, jnp.float32) * scale
    if len(cuts) > 0:
        drawn = steps_of(rng, shape, cuts, -0.22, 0.18) * drawn
    return jnp.clip(drawn, min=-bound, max=bound).astype(kind)


def setup_inputs(seed: int = 0) -> dict:
    arg_keys = jax.random.split(jax.random.key(seed), 9)
    return {
        "queries": draw_queries(jax.random.fold_in(arg_keys[8], 71), 0),
        "new_keys": draw_new_keys(jax.random.fold_in(arg_keys[8], 71), 0),
        "new_values": normal_values(arg_keys[2], (REQS, C, KVH, HD), 1.0, 6.0, ((0, 8), (2, 4))),
        "pool_keys": normal_values(arg_keys[3], (POOL, KVH, PAGE, HD), 1.0, 8.0, ((0, 8), (1, 4))),
        "pool_values": normal_values(arg_keys[4], (POOL, KVH, PAGE, HD), 1.0, 6.0, ((0, 8), (1, 4))),
        "prefix_len": draw_prefix_len(jax.random.fold_in(arg_keys[8], 71), 0),
        "page_table": draw_page_table(jax.random.fold_in(arg_keys[8], 71), 0),
        "out_weight": normal_values(arg_keys[7], (QH * HD, D), (QH * HD) ** -0.5, 0.0625, ((0, 4),)),
    }


def reference(queries, new_keys, new_values, pool_keys, pool_values, prefix_len, page_table, out_weight):
    group_size = QH // KVH
    score_scale = 1.0 / (HD ** 0.5)
    token_ids = jnp.arange(MAXP * PAGE, dtype=jnp.int32)
    positions = jnp.arange(C, dtype=jnp.int32)
    causal = (positions[None, :] <= positions[:, None])[:, None, None, :]

    def one_prompt(inputs):
        query_rows, fresh_keys, fresh_values, length, page_ids = inputs
        safe_pages = jnp.maximum(page_ids, 0)
        keys_prefix = pool_keys[safe_pages].astype(jnp.float32).transpose(1, 0, 2, 3).reshape(KVH, MAXP * PAGE, HD)
        values_prefix = pool_values[safe_pages].astype(jnp.float32).transpose(1, 0, 2, 3).reshape(KVH, MAXP * PAGE, HD)
        seen = (token_ids < length) & jnp.repeat(page_ids >= 0, PAGE)
        seen = seen[None, None, None, :]
        grouped = query_rows.astype(jnp.float32).reshape(C, KVH, group_size, HD)
        prefix_scores = jnp.einsum('cjgd,jkd->cjgk', grouped, keys_prefix) * score_scale
        fresh_scores = jnp.einsum('cjgd,ejd->cjge', grouped, fresh_keys.astype(jnp.float32)) * score_scale
        row_peak = jnp.maximum(jnp.max(jnp.where(seen, prefix_scores, -jnp.inf), axis=-1),
                               jnp.max(jnp.where(causal, fresh_scores, -jnp.inf), axis=-1))
        prefix_weights = jnp.where(seen, jnp.exp(prefix_scores - row_peak[..., None]), 0.0)
        fresh_weights = jnp.where(causal, jnp.exp(fresh_scores - row_peak[..., None]), 0.0)
        weight_sum = jnp.sum(prefix_weights, axis=-1) + jnp.sum(fresh_weights, axis=-1)
        prefix_rounded = lax.optimization_barrier(prefix_weights.astype(jnp.bfloat16)).astype(jnp.float32)
        fresh_rounded = lax.optimization_barrier(fresh_weights.astype(jnp.bfloat16)).astype(jnp.float32)
        weighted = jnp.einsum('cjgk,jkd->cjgd', prefix_rounded, values_prefix)
        weighted = weighted + jnp.einsum('cjge,ejd->cjgd', fresh_rounded, fresh_values.astype(jnp.float32))
        return (weighted / weight_sum[..., None]).astype(jnp.bfloat16).reshape(C, QH * HD)

    attended_heads = lax.map(one_prompt, (queries, new_keys, new_values, prefix_len, page_table))
    flat_heads = attended_heads.reshape(REQS * C, QH * HD)
    group_rows = QH * HD // N_MP
    summed = jnp.zeros((REQS * C, D), jnp.float32)
    for head_group in range(N_MP):
        lower = head_group * group_rows
        partial_value = jnp.dot(flat_heads[:, lower:lower + group_rows], out_weight[lower:lower + group_rows],
                          preferred_element_type=jnp.float32)
        summed = summed + lax.optimization_barrier(partial_value.astype(jnp.bfloat16)).astype(jnp.float32)
    return summed.astype(jnp.bfloat16).reshape(REQS, C, D)
```

```python
import functools
import math

import jax
import jax.numpy as jnp
from jax import lax
from jax.experimental import pallas as pl
from jax.experimental.pallas import tpu as pltpu
from jax.sharding import PartitionSpec as P

MESH = pl.DeviceIdType.MESH
SLOTS = 2
FLOOR = -1e30


def flipped(index, mask, n):
    out, bit = 0, 1
    while bit < n:
        out = out + bit * (((index // bit) + (mask // bit)) % 2)
        bit *= 2
    return out


def line_order(m, n_mp):
    return sorted(range(n_mp), key=lambda d: (-abs(d - m), min(d, n_mp - 1 - d)))


def kernel(
    dims, len_ref, table_ref, nk_ref, nv_ref, q_hbm, pk_hbm, pv_hbm, w_hbm, out_ref,
    pk_ref, pv_ref, q_ref, wbuf, q32, n32, qs, sendk, sendv, recvk, recvv, probs, peaks, sums, acc, attn,
    sbuf, rbuf, own, ids_ref, live_ref,
    in_sem, w_sem, ks_sem, kr_sem, vs_sem, vr_sem, rs_sem, rr_sem,
):
    n, n_mp, tiles, width = dims
    half = n // 2
    fresh = q_ref.shape[1]
    pages, kvh, page, hd = pk_ref.shape
    maxp = table_ref.shape[1]
    group = q_ref.shape[2] // kvh
    lanes = group * fresh
    me = lax.axis_index("seq")
    mz = lax.axis_index("mp")
    side = me % 2
    coef = math.log2(math.e) / math.sqrt(hd)

    loads = [
        pltpu.make_async_copy(src, dst, in_sem.at[i])
        for i, (src, dst) in enumerate(((pk_hbm, pk_ref), (pv_hbm, pv_ref), (q_hbm, q_ref)))
    ]
    orders = [line_order(m, n_mp) for m in range(n_mp)]

    def chunk_at(pos):
        out = jnp.int32(orders[0][pos])
        for m in range(1, n_mp):
            out = jnp.where(mz == m, orders[m][pos], out)
        return out

    def w_copy(pos, t):
        col = pl.multiple_of((chunk_at(pos) * tiles + t) * width, 128)
        i = pos * tiles + t
        return pltpu.make_async_copy(w_hbm.at[:, pl.ds(col, width)], wbuf.at[i], w_sem.at[i])

    barrier = pltpu.get_barrier_semaphore()
    for k in range(1, n):
        pl.semaphore_signal(
            barrier, inc=1, device_id={"seq": flipped(me, k, n)}, device_id_type=MESH
        )

    @pl.when(mz > 0)
    def _():
        pl.semaphore_signal(barrier, inc=1, device_id={"mp": mz - 1}, device_id_type=MESH)

    @pl.when(mz < n_mp - 1)
    def _():
        pl.semaphore_signal(barrier, inc=1, device_id={"mp": mz + 1}, device_id_type=MESH)

    for load in loads:
        load.start()

    def scan(row, owner):
        first, count = owner * pages, 0
        ids = [0] * SLOTS
        live = [0] * SLOTS
        length = len_ref[row]
        for l in range(maxp):
            p = table_ref[row, l]
            owned = (p >= first) & (p < first + pages)
            room = jnp.clip(length - l * page, 0, page)
            for s in range(SLOTS):
                here = owned & (count == s)
                ids[s] = jnp.where(here, p - first, ids[s])
                live[s] = jnp.where(here, room, live[s])
            count = count + owned.astype(jnp.int32)
        return ids, live

    def find(k, _):
        other = flipped(me, k, n)
        ids, _ = scan(other, me)
        _, live = scan(me, other)
        for s in range(SLOTS):
            ids_ref[k * SLOTS + s] = ids[s]
            live_ref[k * SLOTS + s] = live[s]
        return 0

    lax.fori_loop(0, n, find, 0)

    def page_copy(send, recv, s_sem, r_sem, k):
        return pltpu.make_async_remote_copy(
            src_ref=send.at[k], dst_ref=recv.at[k], send_sem=s_sem.at[k],
            recv_sem=r_sem.at[k], device_id={"seq": flipped(me, k, n)}, device_id_type=MESH,
        )

    def k_copy(k):
        return page_copy(sendk, recvk, ks_sem, kr_sem, k)

    def v_copy(k):
        return page_copy(sendv, recvv, vs_sem, vr_sem, k)

    def targets(phase, act):
        off = (side + phase) % 2

        def one(i, _):
            act(2 * (half - 1 - i) + off)
            return 0

        lax.fori_loop(0, half - 1 + off, one, 0)

    def pack(pool, send):
        def one(k):
            for s in range(SLOTS):
                for j in range(kvh):
                    send[k, j, s] = pool[ids_ref[k * SLOTS + s], j]
        return one

    loads[0].wait()
    targets(0, pack(pk_ref, sendk))
    around = jnp.where(mz > 0, 1, 0) + jnp.where(mz < n_mp - 1, 1, 0)
    pl.semaphore_wait(barrier, n - 1 + around)
    targets(0, lambda k: k_copy(k).start())
    loads[1].wait()
    targets(0, pack(pv_ref, sendv))
    targets(0, lambda k: v_copy(k).start())
    targets(1, pack(pk_ref, sendk))
    targets(1, pack(pv_ref, sendv))
    pack(pk_ref, recvk)(0)
    pack(pv_ref, recvv)(0)
    loads[2].wait()
    for pos in range(n_mp):
        for t in range(tiles):
            w_copy(pos, t).start()

    q32[...] = q_ref[0].astype(jnp.float32)
    n32[0] = nk_ref[0].astype(jnp.float32)
    n32[1] = nv_ref[0].astype(jnp.float32)
    for h in range(kvh * group):
        j, g = h // group, h % group
        qs[j, g * fresh:(g + 1) * fresh, :] = q32[:, h, :].astype(jnp.bfloat16)

    def scores(keys, j):
        return lax.dot_general(
            keys, qs[j], (((1,), (1,)), ((), ())), preferred_element_type=jnp.float32
        )

    def mixed(values, weights):
        return lax.dot_general(
            values, weights, (((0,), (0,)), ((), ())), preferred_element_type=jnp.float32
        )

    lane = lax.broadcasted_iota(jnp.int32, (fresh, lanes), 1)
    token = lane
    for g in range(1, group):
        token = token - jnp.where(lane >= g * fresh, fresh, 0)
    causal = lax.broadcasted_iota(jnp.int32, (fresh, lanes), 0) <= token
    for j in range(kvh):
        s = jnp.where(causal, scores(n32[0, :, j, :].astype(jnp.bfloat16), j), FLOOR)
        m = jnp.max(s, axis=0, keepdims=True)
        w = jnp.exp2((s - m) * coef)
        peaks[n, j] = m
        sums[n, j] = jnp.sum(w, axis=0, keepdims=True)
        acc[j] = mixed(n32[1, :, j, :].astype(jnp.bfloat16), w.astype(jnp.bfloat16))

    def second_phase():
        targets(0, lambda k: k_copy(k).wait_send())
        targets(0, lambda k: v_copy(k).wait_send())
        targets(1, lambda k: k_copy(k).start())
        targets(1, lambda k: v_copy(k).start())

    @pl.when(side == 1)
    def _():
        second_phase()

    def score_block(k, _):
        @pl.when(k > 0)
        def _():
            k_copy(k).wait_recv()

        row = lax.broadcasted_iota(jnp.int32, (SLOTS * page, lanes), 0)
        allowed = row < live_ref[k * SLOTS]
        for s in range(1, SLOTS):
            allowed = allowed | ((row >= s * page) & (row < s * page + live_ref[k * SLOTS + s]))
        for j in range(kvh):
            s = scores(recvk[k, j].reshape(SLOTS * page, hd), j)
            s = jnp.where(allowed, s, FLOOR)
            m = jnp.max(s, axis=0, keepdims=True)
            w = jnp.exp2((s - m) * coef)
            peaks[k, j] = m
            sums[k, j] = jnp.sum(w, axis=0, keepdims=True)
            probs[k, j] = w.astype(jnp.bfloat16)
        return 0

    lax.fori_loop(0, n, score_block, 0)

    for j in range(kvh):
        top = peaks[n, j]
        for k in range(n):
            top = jnp.maximum(top, peaks[k, j])
        total = jnp.zeros_like(top)
        for k in range(n + 1):
            total = total + sums[k, j] * jnp.exp2((peaks[k, j] - top) * coef)
        acc[j] = acc[j] * jnp.exp2((peaks[n, j] - top) * coef)
        sums[n, j] = total
        peaks[n, j] = top

    def value_block(k, _):
        @pl.when(k > 0)
        def _():
            v_copy(k).wait_recv()

        for j in range(kvh):
            part = mixed(recvv[k, j].reshape(SLOTS * page, hd), probs[k, j])
            acc[j] = acc[j] + part * jnp.exp2((peaks[k, j] - peaks[n, j]) * coef)
        return 0

    lax.fori_loop(0, n, value_block, 0)

    @pl.when(side == 0)
    def _():
        second_phase()

    for j in range(kvh):
        heads = (acc[j] / sums[n, j]).T.astype(jnp.bfloat16)
        for g in range(group):
            h = j * group + g
            attn[:, h * hd:(h + 1) * hd] = heads[g * fresh:(g + 1) * fresh, :]

    def sum_copy(pos, t):
        d = chunk_at(pos)
        step = jnp.where(d > mz, 1, -1)
        slot = jnp.where(d == mz - 1, n_mp, d)
        return pltpu.make_async_remote_copy(
            src_ref=sbuf.at[pos, t], dst_ref=rbuf.at[slot, t], send_sem=rs_sem.at[pos, t],
            recv_sem=rr_sem.at[slot, t], device_id={"mp": mz + step}, device_id_type=MESH,
        )

    def arrival(slot, t, source):
        return pltpu.make_async_remote_copy(
            src_ref=sbuf.at[0, t], dst_ref=rbuf.at[slot, t], send_sem=rs_sem.at[0, t],
            recv_sem=rr_sem.at[slot, t], device_id={"mp": source}, device_id_type=MESH,
        )

    def product(pos, t):
        i = pos * tiles + t
        pltpu.make_async_copy(w_hbm.at[:, pl.ds(0, width)], wbuf.at[i], w_sem.at[i]).wait()
        return jnp.dot(attn[...], wbuf[i], preferred_element_type=jnp.float32)

    for pos in range(n_mp - 1):
        d = chunk_at(pos)
        outer = ((d > mz) & (mz > 0)) | ((d < mz) & (mz < n_mp - 1))
        source = jnp.where(d > mz, mz - 1, mz + 1)

        def project(t, _, pos=pos, d=d, outer=outer, source=source):
            part = product(pos, t)

            @pl.when(outer)
            def _():
                arrival(d, t, source).wait_recv()
                sbuf[pos, t] = (part + rbuf[d, t].astype(jnp.float32)).astype(jnp.bfloat16)

            @pl.when(jnp.logical_not(outer))
            def _():
                sbuf[pos, t] = part.astype(jnp.bfloat16)

            sum_copy(pos, t).start()
            return 0

        lax.fori_loop(0, tiles, project, 0)

    def project_own(t, _):
        own[t] = product(n_mp - 1, t)
        return 0

    lax.fori_loop(0, tiles, project_own, 0)

    for t in range(tiles):
        @pl.when(mz > 0)
        def _(t=t):
            arrival(mz, t, mz - 1).wait_recv()
            own[t] = own[t] + rbuf[mz, t].astype(jnp.float32)

        @pl.when(mz < n_mp - 1)
        def _(t=t):
            arrival(n_mp, t, mz + 1).wait_recv()
            own[t] = own[t] + rbuf[n_mp, t].astype(jnp.float32)

        out_ref[:, t * width:(t + 1) * width] = own[t].astype(out_ref.dtype)

    targets(1, lambda k: k_copy(k).wait_send())
    targets(1, lambda k: v_copy(k).wait_send())
    for pos in range(n_mp - 1):
        for t in range(tiles):
            sum_copy(pos, t).wait_send()


def on_device(
    n, n_mp, queries, new_keys, new_values, pool_keys, pool_values, prefix_len, page_table, out_weight
):
    reqs, fresh, heads, hd = queries.shape
    pages, kvh, page, _ = pool_keys.shape
    lanes = heads // kvh * fresh
    depth, model = out_weight.shape
    chunk = model // n_mp
    width = min(512, chunk)
    tiles = chunk // width
    bf16, f32 = jnp.bfloat16, jnp.float32
    dma = pltpu.SemaphoreType.DMA
    vmem = pl.BlockSpec(memory_space=pltpu.VMEM)
    smem = pl.BlockSpec(memory_space=pltpu.SMEM)
    pages_shape = (n, kvh, SLOTS, page, hd)
    out = pl.pallas_call(
        functools.partial(kernel, (n, n_mp, tiles, width)),
        out_shape=jax.ShapeDtypeStruct((fresh, chunk), bf16),
        in_specs=[smem, smem, vmem, vmem] + [pl.BlockSpec(memory_space=pl.ANY)] * 4,
        out_specs=vmem,
        scratch_shapes=[
            pltpu.VMEM(pool_keys.shape, bf16),
            pltpu.VMEM(pool_values.shape, bf16),
            pltpu.VMEM(queries.shape, bf16),
            pltpu.VMEM((n_mp * tiles, depth, width), bf16),
            pltpu.VMEM((fresh, heads, hd), f32),
            pltpu.VMEM((2, fresh, kvh, hd), f32),
            pltpu.VMEM((kvh, lanes, hd), bf16),
            pltpu.VMEM(pages_shape, bf16),
            pltpu.VMEM(pages_shape, bf16),
            pltpu.VMEM(pages_shape, bf16),
            pltpu.VMEM(pages_shape, bf16),
            pltpu.VMEM((n, kvh, SLOTS * page, lanes), bf16),
            pltpu.VMEM((n + 1, kvh, 1, lanes), f32),
            pltpu.VMEM((n + 1, kvh, 1, lanes), f32),
            pltpu.VMEM((kvh, hd, lanes), f32),
            pltpu.VMEM((fresh, depth), bf16),
            pltpu.VMEM((n_mp, tiles, fresh, width), bf16),
            pltpu.VMEM((n_mp + 1, tiles, fresh, width), bf16),
            pltpu.VMEM((tiles, fresh, width), f32),
            pltpu.SMEM((n * SLOTS,), jnp.int32),
            pltpu.SMEM((n * SLOTS,), jnp.int32),
            dma((3,)),
            dma((n_mp * tiles,)),
            dma((n,)), dma((n,)), dma((n,)), dma((n,)),
            dma((n_mp, tiles)), dma((n_mp + 1, tiles)),
        ],
        compiler_params=pltpu.CompilerParams(
            collective_id=0, has_side_effects=True, vmem_limit_bytes=60 * 2**20
        ),
    )(
        prefix_len,
        page_table,
        new_keys,
        new_values,
        queries,
        pool_keys,
        pool_values,
        out_weight,
    )
    return out[None]


def solution(mesh):
    in_specs = (
        P("seq", None, "mp", None),
        P("seq", None, "mp", None),
        P("seq", None, "mp", None),
        P("seq", "mp", None, None),
        P("seq", "mp", None, None),
        P(),
        P(),
        P("mp", None),
    )
    body = functools.partial(on_device, mesh.shape["seq"], mesh.shape["mp"])
    return jax.shard_map(
        body, mesh=mesh, in_specs=in_specs, out_specs=P("seq", None, "mp"), check_vma=False
    )
```

```python
import functools
import math

import jax
import jax.numpy as jnp
from jax import lax
from jax.experimental import pallas as pl
from jax.experimental.pallas import tpu as pltpu
from jax.sharding import PartitionSpec as P

MESH = pl.DeviceIdType.MESH
SLOTS = 2
FLOOR = -1e30


def flipped(index, mask, n):
    out, bit = 0, 1
    while bit < n:
        out = out + bit * (((index // bit) + (mask // bit)) % 2)
        bit *= 2
    return out


def line_order(m, n_mp):
    ranked = sorted(range(n_mp), key=lambda d: (-abs(d - m), min(d, n_mp - 1 - d)))
    if 0 < m < n_mp - 1:
        return ranked[-1:] + ranked[:-1]
    return ranked


def kernel(
    dims, len_hbm, table_hbm, nk_hbm, nv_hbm, q_hbm, pk_hbm, pv_hbm, w_hbm, out_hbm,
    len_ref, table_ref, nk_ref, nv_ref, pk_ref, pv_ref, q_ref, out_ref,
    wbuf, q32, n32, qs, bias, sendk, sendv, recvk, recvv, probs, peaks, sums, acc, attn,
    sbuf, rbuf, own, ids_ref, live_ref,
    in_sem, out_sem, w_sem, ks_sem, kr_sem, vs_sem, vr_sem, rs_sem, rr_sem,
):
    n, n_mp, tiles, width = dims
    half = n // 2
    fresh = q_ref.shape[1]
    pages, kvh, page, hd = pk_ref.shape
    maxp = table_ref.shape[1]
    group = q_ref.shape[2] // kvh
    lanes = group * fresh
    me = lax.axis_index("seq")
    mz = lax.axis_index("mp")
    side = me % 2
    coef = math.log2(math.e) / math.sqrt(hd)

    loads = [
        pltpu.make_async_copy(src, dst, in_sem.at[i])
        for i, (src, dst) in enumerate((
            (len_hbm, len_ref), (table_hbm, table_ref), (pk_hbm, pk_ref), (pv_hbm, pv_ref),
            (q_hbm, q_ref), (nk_hbm, nk_ref), (nv_hbm, nv_ref),
        ))
    ]
    orders = [line_order(m, n_mp) for m in range(n_mp)]

    def chunk_at(pos):
        out = jnp.int32(orders[0][pos])
        for m in range(1, n_mp):
            out = jnp.where(mz == m, orders[m][pos], out)
        return out

    def w_copy(pos, t):
        col = pl.multiple_of((chunk_at(pos) * tiles + t) * width, 128)
        i = pos * tiles + t
        return pltpu.make_async_copy(w_hbm.at[:, pl.ds(col, width)], wbuf.at[i], w_sem.at[i])

    barrier = pltpu.get_barrier_semaphore()
    for k in range(1, n):
        pl.semaphore_signal(
            barrier, inc=1, device_id={"seq": flipped(me, k, n)}, device_id_type=MESH
        )

    @pl.when(mz > 0)
    def _():
        pl.semaphore_signal(barrier, inc=1, device_id={"mp": mz - 1}, device_id_type=MESH)

    @pl.when(mz < n_mp - 1)
    def _():
        pl.semaphore_signal(barrier, inc=1, device_id={"mp": mz + 1}, device_id_type=MESH)

    for load in loads:
        load.start()

    def scan(row, owner):
        first, count = owner * pages, 0
        ids = [0] * SLOTS
        live = [0] * SLOTS
        length = len_ref[row]
        for l in range(maxp):
            p = table_ref[row, l]
            owned = (p >= first) & (p < first + pages)
            room = jnp.clip(length - l * page, 0, page)
            for s in range(SLOTS):
                here = owned & (count == s)
                ids[s] = jnp.where(here, p - first, ids[s])
                live[s] = jnp.where(here, room, live[s])
            count = count + owned.astype(jnp.int32)
        return ids, live

    def find(k, _):
        other = flipped(me, k, n)
        ids, _ = scan(other, me)
        _, live = scan(me, other)
        for s in range(SLOTS):
            ids_ref[k * SLOTS + s] = ids[s]
            live_ref[k * SLOTS + s] = live[s]
        return 0

    loads[0].wait()
    loads[1].wait()
    lax.fori_loop(0, n, find, 0)

    homes = []
    for q in range(half):
        home, bit = me - side, 2
        while bit < n:
            if 2 * q & bit:
                home = home + jnp.where(lax.rem(lax.div(me, bit), 2) == 0, bit, -bit)
            bit *= 2
        homes.append(home)

    def page_copy(send, recv, s_sem, r_sem, k, j, target):
        return pltpu.make_async_remote_copy(
            src_ref=send.at[j, k], dst_ref=recv.at[j, k], send_sem=s_sem.at[k, j],
            recv_sem=r_sem.at[k, j], device_id={"seq": target}, device_id_type=MESH,
        )

    def k_copy(k, j, target):
        return page_copy(sendk, recvk, ks_sem, kr_sem, k, j, target)

    def v_copy(k, j, target):
        return page_copy(sendv, recvv, vs_sem, vr_sem, k, j, target)

    def targets(phase, act):
        off = side if phase == 0 else 1 - side
        for q in reversed(range(1, half)):
            act(2 * q + off, homes[q] + phase)

        @pl.when(side != phase)
        def _():
            act(1, homes[0] + phase)

    def pack(pool, send):
        def one(k, target):
            for s in range(SLOTS):
                for j in range(kvh):
                    send[j, k, s] = pool[ids_ref[k * SLOTS + s], j]
        return one

    def start(phase, copy):
        for j in range(kvh):
            targets(phase, lambda k, target: copy(k, j, target).start())

    def sent(phase):
        for copy in (k_copy, v_copy):
            for j in range(kvh):
                targets(phase, lambda k, target: copy(k, j, target).wait_send())

    loads[2].wait()
    targets(0, pack(pk_ref, sendk))
    around = jnp.where(mz > 0, 1, 0) + jnp.where(mz < n_mp - 1, 1, 0)
    pl.semaphore_wait(barrier, n - 1 + around)
    start(0, k_copy)
    loads[3].wait()
    targets(0, pack(pv_ref, sendv))
    start(0, v_copy)
    targets(1, pack(pk_ref, sendk))
    targets(1, pack(pv_ref, sendv))
    pack(pk_ref, recvk)(0, me)
    pack(pv_ref, recvv)(0, me)
    for i in range(4, 7):
        loads[i].wait()
    for pos in range(n_mp):
        for t in range(tiles):
            w_copy(pos, t).start()

    row = lax.broadcasted_iota(jnp.int32, (SLOTS * page, hd), 0)

    def mask(k, _):
        allowed = row < live_ref[k * SLOTS]
        for i in range(1, SLOTS):
            allowed = allowed | ((row >= i * page) & (row < i * page + live_ref[k * SLOTS + i]))
        bias[k] = jnp.where(allowed, 0.0, FLOOR).astype(jnp.bfloat16)
        return 0

    lax.fori_loop(0, n, mask, 0)
    unit = jnp.where(lax.broadcasted_iota(jnp.int32, (lanes, hd), 1) == 0, 1.0, 0.0).astype(jnp.bfloat16)
    for j in range(kvh):
        qs[j, :, hd:] = unit
    q32[...] = q_ref[0].astype(jnp.float32)
    n32[0] = nk_ref[0].astype(jnp.float32)
    n32[1] = nv_ref[0].astype(jnp.float32)
    for h in range(kvh * group):
        j, g = h // group, h % group
        qs[j, g * fresh:(g + 1) * fresh, :hd] = q32[:, h, :].astype(jnp.bfloat16)

    def scores(keys, queries):
        return lax.dot_general(
            keys, queries, (((1,), (1,)), ((), ())), preferred_element_type=jnp.float32
        )

    def mixed(values, weights):
        return lax.dot_general(
            values, weights, (((0,), (0,)), ((), ())), preferred_element_type=jnp.float32
        )

    lane = lax.broadcasted_iota(jnp.int32, (fresh, lanes), 1)
    token = lane
    for g in range(1, group):
        token = token - jnp.where(lane >= g * fresh, fresh, 0)
    causal = lax.broadcasted_iota(jnp.int32, (fresh, lanes), 0) <= token
    for j in range(kvh):
        s = jnp.where(causal, scores(n32[0, :, j, :].astype(jnp.bfloat16), qs[j, :, :hd]), FLOOR)
        m = jnp.max(s, axis=0, keepdims=True)
        w = jnp.exp2((s - m) * coef)
        peaks[half, j] = m
        sums[half, j] = jnp.sum(w, axis=0, keepdims=True)
        acc[j] = mixed(n32[1, :, j, :].astype(jnp.bfloat16), w.astype(jnp.bfloat16))

    def second_phase():
        sent(0)
        start(1, k_copy)
        start(1, v_copy)

    @pl.when(side == 1)
    def _():
        second_phase()

    def arrived(copy, i, j):
        @pl.when(i > 0)
        def _():
            copy(2 * i, j, homes[1]).wait_recv()

        copy(2 * i + 1, j, homes[1]).wait_recv()

    for j in range(kvh):
        def score_block(i, _, j=j):
            arrived(k_copy, i, j)
            s = scores(recvk[j, pl.ds(2 * i, 2)].reshape(2 * SLOTS * page, hd), qs[j, :, :hd])
            b = bias[pl.ds(2 * i, 2)].reshape(2 * SLOTS * page, hd).astype(jnp.float32)
            s = s + jnp.concatenate([b] * (lanes // hd), axis=1)
            m = jnp.max(s, axis=0, keepdims=True)
            w = jnp.exp2((s - m) * coef)
            peaks[i, j] = m
            sums[i, j] = jnp.sum(w, axis=0, keepdims=True)
            probs[i, j] = w.astype(jnp.bfloat16)
            return 0

        lax.fori_loop(0, half, score_block, 0)

    for j in range(kvh):
        top = peaks[half, j]
        for i in range(half):
            top = jnp.maximum(top, peaks[i, j])
        total = jnp.zeros_like(top)
        for i in range(half + 1):
            scale = jnp.exp2((peaks[i, j] - top) * coef)
            total = total + sums[i, j] * scale
            peaks[i, j] = scale
        acc[j] = acc[j] * peaks[half, j]
        sums[half, j] = total

        def value_block(i, _, j=j):
            arrived(v_copy, i, j)
            part = mixed(recvv[j, pl.ds(2 * i, 2)].reshape(2 * SLOTS * page, hd), probs[i, j])
            acc[j] = acc[j] + part * peaks[i, j]
            return 0

        lax.fori_loop(0, half, value_block, 0)

    @pl.when(side == 0)
    def _():
        second_phase()

    for j in range(kvh):
        heads = (acc[j] / sums[half, j]).T.astype(jnp.bfloat16)
        for g in range(group):
            h = j * group + g
            attn[:, h * hd:(h + 1) * hd] = heads[g * fresh:(g + 1) * fresh, :]

    def out_copy(t):
        return pltpu.make_async_copy(
            out_ref.at[t], out_hbm.at[:, pl.ds(t * width, width)], out_sem.at[t]
        )

    def sum_copy(pos, t):
        d = chunk_at(pos)
        step = jnp.where(d > mz, 1, -1)
        slot = jnp.where(d == mz - 1, n_mp, d)
        return pltpu.make_async_remote_copy(
            src_ref=sbuf.at[pos, t], dst_ref=rbuf.at[slot, t], send_sem=rs_sem.at[pos, t],
            recv_sem=rr_sem.at[slot, t], device_id={"mp": mz + step}, device_id_type=MESH,
        )

    def arrival(slot, t, source):
        return pltpu.make_async_remote_copy(
            src_ref=sbuf.at[0, t], dst_ref=rbuf.at[slot, t], send_sem=rs_sem.at[0, t],
            recv_sem=rr_sem.at[slot, t], device_id={"mp": source}, device_id_type=MESH,
        )

    def product(pos, t):
        i = pos * tiles + t
        pltpu.make_async_copy(w_hbm.at[:, pl.ds(0, width)], wbuf.at[i], w_sem.at[i]).wait()
        return jnp.dot(attn[...], wbuf[i], preferred_element_type=jnp.float32)

    def project(pos, t):
        d = chunk_at(pos)
        part = product(pos, t)
        relay = ((d > mz) & (mz > 0)) | ((d < mz) & (mz < n_mp - 1))

        @pl.when(d == mz)
        def _():
            own[t] = part

        @pl.when((d != mz) & relay)
        def _():
            arrival(d, t, jnp.where(d > mz, mz - 1, mz + 1)).wait_recv()
            sbuf[pos, t] = (part + rbuf[d, t].astype(jnp.float32)).astype(jnp.bfloat16)

        @pl.when((d != mz) & jnp.logical_not(relay))
        def _():
            sbuf[pos, t] = part.astype(jnp.bfloat16)

        @pl.when(d != mz)
        def _():
            sum_copy(pos, t).start()

    for group_of in [(pos,) for pos in range(n_mp - 2)] + [(n_mp - 2, n_mp - 1)]:
        def step(t, _, group_of=group_of):
            for pos in group_of:
                project(pos, t)
            return 0

        lax.fori_loop(0, tiles, step, 0)

    for t in range(tiles):
        @pl.when(mz > 0)
        def _(t=t):
            arrival(mz, t, mz - 1).wait_recv()
            own[t] = own[t] + rbuf[mz, t].astype(jnp.float32)

        @pl.when(mz < n_mp - 1)
        def _(t=t):
            arrival(n_mp, t, mz + 1).wait_recv()
            own[t] = own[t] + rbuf[n_mp, t].astype(jnp.float32)

        out_ref[t] = own[t].astype(out_ref.dtype)
        out_copy(t).start()

    sent(1)
    for pos in range(n_mp):
        @pl.when(chunk_at(pos) != mz)
        def _(pos=pos):
            for t in range(tiles):
                sum_copy(pos, t).wait_send()

    for t in range(tiles):
        out_copy(t).wait()


def on_device(
    n, n_mp, queries, new_keys, new_values, pool_keys, pool_values, prefix_len, page_table, out_weight
):
    reqs, fresh, heads, hd = queries.shape
    pages, kvh, page, _ = pool_keys.shape
    lanes = heads // kvh * fresh
    depth, model = out_weight.shape
    chunk = model // n_mp
    width = min(512, chunk)
    tiles = chunk // width
    bf16, f32 = jnp.bfloat16, jnp.float32
    dma = pltpu.SemaphoreType.DMA
    pages_shape = (kvh, n, SLOTS, page, hd)
    out = pl.pallas_call(
        functools.partial(kernel, (n, n_mp, tiles, width)),
        out_shape=jax.ShapeDtypeStruct((fresh, chunk), bf16),
        in_specs=[pl.BlockSpec(memory_space=pl.ANY)] * 8,
        out_specs=pl.BlockSpec(memory_space=pl.ANY),
        scratch_shapes=[
            pltpu.SMEM(prefix_len.shape, jnp.int32),
            pltpu.SMEM(page_table.shape, jnp.int32),
            pltpu.VMEM(new_keys.shape, bf16),
            pltpu.VMEM(new_values.shape, bf16),
            pltpu.VMEM(pool_keys.shape, bf16),
            pltpu.VMEM(pool_values.shape, bf16),
            pltpu.VMEM(queries.shape, bf16),
            pltpu.VMEM((tiles, fresh, width), bf16),
            pltpu.VMEM((n_mp * tiles, depth, width), bf16),
            pltpu.VMEM((fresh, heads, hd), f32),
            pltpu.VMEM((2, fresh, kvh, hd), f32),
            pltpu.VMEM((kvh, lanes, 2 * hd), bf16),
            pltpu.VMEM((n, SLOTS * page, hd), bf16),
            pltpu.VMEM(pages_shape, bf16),
            pltpu.VMEM(pages_shape, bf16),
            pltpu.VMEM(pages_shape, bf16),
            pltpu.VMEM(pages_shape, bf16),
            pltpu.VMEM((n // 2, kvh, 2 * SLOTS * page, lanes), bf16),
            pltpu.VMEM((n // 2 + 1, kvh, 1, lanes), f32),
            pltpu.VMEM((n // 2 + 1, kvh, 1, lanes), f32),
            pltpu.VMEM((kvh, hd, lanes), f32),
            pltpu.VMEM((fresh, depth), bf16),
            pltpu.VMEM((n_mp, tiles, fresh, width), bf16),
            pltpu.VMEM((n_mp + 1, tiles, fresh, width), bf16),
            pltpu.VMEM((tiles, fresh, width), f32),
            pltpu.SMEM((n * SLOTS,), jnp.int32),
            pltpu.SMEM((n * SLOTS,), jnp.int32),
            dma((7,)),
            dma((tiles,)),
            dma((n_mp * tiles,)),
            dma((n, kvh)), dma((n, kvh)), dma((n, kvh)), dma((n, kvh)),
            dma((n_mp, tiles)), dma((n_mp + 1, tiles)),
        ],
        compiler_params=pltpu.CompilerParams(
            collective_id=0, has_side_effects=True, vmem_limit_bytes=60 * 2**20
        ),
    )(
        prefix_len,
        page_table,
        new_keys,
        new_values,
        queries,
        pool_keys,
        pool_values,
        out_weight,
    )
    return out[None]


def solution(mesh):
    in_specs = (
        P("seq", None, "mp", None),
        P("seq", None, "mp", None),
        P("seq", None, "mp", None),
        P("seq", "mp", None, None),
        P("seq", "mp", None, None),
        P(),
        P(),
        P("mp", None),
    )
    body = functools.partial(on_device, mesh.shape["seq"], mesh.shape["mp"])
    return jax.shard_map(
        body, mesh=mesh, in_specs=in_specs, out_specs=P("seq", None, "mp"), check_vma=False
    )
```

```python
import functools
import math

import jax
import jax.numpy as jnp
from jax import lax
from jax.experimental import pallas as pl
from jax.experimental.pallas import tpu as pltpu
from jax.sharding import PartitionSpec as P

MESH = pl.DeviceIdType.MESH
SLOTS = 2
FLOOR = -1e30


def flipped(index, mask, n):
    out, bit = 0, 1
    while bit < n:
        out = out + bit * (((index // bit) + (mask // bit)) % 2)
        bit *= 2
    return out


def line_order(m, n_mp):
    ranked = sorted(range(n_mp), key=lambda d: (-abs(d - m), min(d, n_mp - 1 - d)))
    if 0 < m < n_mp - 1:
        return ranked[-1:] + ranked[:-1]
    return ranked


def kernel(
    dims, len_hbm, table_hbm, nk_hbm, nv_hbm, q_hbm, pk_hbm, pv_hbm, w_hbm, out_ref,
    len_ref, table_ref, nk_ref, nv_ref, pk_ref, pv_ref, q_ref,
    wbuf, q32, n32, qs, bias, sendk, sendv, recvk, recvv, probs, peaks, sums, acc, attn,
    sbuf, rbuf, own, ids_ref, live_ref,
    in_sem, w_sem, ks_sem, kr_sem, vs_sem, vr_sem, rs_sem, rr_sem,
):
    n, n_mp, tiles, width = dims
    half = n // 2
    held = (n_mp - 1) * tiles
    fresh = q_ref.shape[1]
    pages, kvh, page, hd = pk_ref.shape
    maxp = table_ref.shape[1]
    group = q_ref.shape[2] // kvh
    lanes = group * fresh
    me = lax.axis_index("seq")
    mz = lax.axis_index("mp")
    side = me % 2
    coef = math.log2(math.e) / math.sqrt(hd)

    loads = [
        pltpu.make_async_copy(src, dst, in_sem.at[i])
        for i, (src, dst) in enumerate((
            (len_hbm, len_ref), (table_hbm, table_ref), (pk_hbm, pk_ref), (pv_hbm, pv_ref),
            (q_hbm, q_ref), (nk_hbm, nk_ref), (nv_hbm, nv_ref),
        ))
    ]
    orders = [line_order(m, n_mp) for m in range(n_mp)]

    def chunk_at(pos):
        out = jnp.int32(orders[0][pos])
        for m in range(1, n_mp):
            out = jnp.where(mz == m, orders[m][pos], out)
        return out

    def w_copy(pos, t):
        col = pl.multiple_of((chunk_at(pos) * tiles + t) * width, 128)
        i = pos * tiles + t
        return pltpu.make_async_copy(w_hbm.at[:, pl.ds(col, width)], wbuf.at[i % held], w_sem.at[i])

    barrier = pltpu.get_barrier_semaphore()
    for k in range(1, n):
        pl.semaphore_signal(
            barrier, inc=1, device_id={"seq": flipped(me, k, n)}, device_id_type=MESH
        )

    @pl.when(mz > 0)
    def _():
        pl.semaphore_signal(barrier, inc=1, device_id={"mp": mz - 1}, device_id_type=MESH)

    @pl.when(mz < n_mp - 1)
    def _():
        pl.semaphore_signal(barrier, inc=1, device_id={"mp": mz + 1}, device_id_type=MESH)

    for load in loads:
        load.start()

    def scan(row, owner):
        first, count = owner * pages, 0
        ids = [0] * SLOTS
        live = [0] * SLOTS
        length = len_ref[row]
        for l in range(maxp):
            p = table_ref[row, l]
            owned = (p >= first) & (p < first + pages)
            room = jnp.clip(length - l * page, 0, page)
            for s in range(SLOTS):
                here = owned & (count == s)
                ids[s] = jnp.where(here, p - first, ids[s])
                live[s] = jnp.where(here, room, live[s])
            count = count + owned.astype(jnp.int32)
        return ids, live

    def find(k, _):
        other = flipped(me, k, n)
        ids, _ = scan(other, me)
        _, live = scan(me, other)
        for s in range(SLOTS):
            ids_ref[k * SLOTS + s] = ids[s]
            live_ref[k * SLOTS + s] = live[s]
        return 0

    loads[0].wait()
    loads[1].wait()
    lax.fori_loop(0, n, find, 0)

    homes = []
    for q in range(half):
        home, bit = me - side, 2
        while bit < n:
            if 2 * q & bit:
                home = home + jnp.where(lax.rem(lax.div(me, bit), 2) == 0, bit, -bit)
            bit *= 2
        homes.append(home)

    def page_copy(send, recv, s_sem, r_sem, k, j, target):
        return pltpu.make_async_remote_copy(
            src_ref=send.at[j, k], dst_ref=recv.at[j, k], send_sem=s_sem.at[k, j],
            recv_sem=r_sem.at[k, j], device_id={"seq": target}, device_id_type=MESH,
        )

    def k_copy(k, j, target):
        return page_copy(sendk, recvk, ks_sem, kr_sem, k, j, target)

    def v_copy(k, j, target):
        return page_copy(sendv, recvv, vs_sem, vr_sem, k, j, target)

    def targets(phase, act):
        off = side if phase == 0 else 1 - side
        for q in reversed(range(1, half)):
            act(2 * q + off, homes[q] + phase)

        @pl.when(side != phase)
        def _():
            act(1, homes[0] + phase)

    def pack(pool, send):
        def one(k, target):
            for s in range(SLOTS):
                for j in range(kvh):
                    send[j, k, s] = pool[ids_ref[k * SLOTS + s], j]
        return one

    def start(phase, copy):
        for j in range(kvh):
            targets(phase, lambda k, target: copy(k, j, target).start())

    def sent(phase):
        for copy in (k_copy, v_copy):
            for j in range(kvh):
                targets(phase, lambda k, target: copy(k, j, target).wait_send())

    loads[2].wait()
    targets(0, pack(pk_ref, sendk))
    around = jnp.where(mz > 0, 1, 0) + jnp.where(mz < n_mp - 1, 1, 0)
    pl.semaphore_wait(barrier, n - 1 + around)
    start(0, k_copy)
    loads[3].wait()
    targets(0, pack(pv_ref, sendv))
    start(0, v_copy)
    targets(1, pack(pk_ref, sendk))
    targets(1, pack(pv_ref, sendv))
    pack(pk_ref, recvk)(0, me)
    pack(pv_ref, recvv)(0, me)
    for i in range(4, 7):
        loads[i].wait()
    for pos in range(n_mp - 1):
        for t in range(tiles):
            w_copy(pos, t).start()

    row = lax.broadcasted_iota(jnp.int32, (SLOTS * page, hd), 0)

    def mask(k, _):
        allowed = row < live_ref[k * SLOTS]
        for i in range(1, SLOTS):
            allowed = allowed | ((row >= i * page) & (row < i * page + live_ref[k * SLOTS + i]))
        bias[k] = jnp.where(allowed, 0.0, FLOOR).astype(jnp.bfloat16)
        return 0

    lax.fori_loop(0, n, mask, 0)
    q32[...] = q_ref[0].astype(jnp.float32)
    n32[0] = nk_ref[0].astype(jnp.float32)
    n32[1] = nv_ref[0].astype(jnp.float32)
    for h in range(kvh * group):
        j, g = h // group, h % group
        qs[j, g * fresh:(g + 1) * fresh, :] = q32[:, h, :].astype(jnp.bfloat16)

    def scores(keys, queries):
        return lax.dot_general(
            keys, queries, (((1,), (1,)), ((), ())), preferred_element_type=jnp.float32
        )

    def mixed(values, weights):
        return lax.dot_general(
            values, weights, (((0,), (0,)), ((), ())), preferred_element_type=jnp.float32
        )

    lane = lax.broadcasted_iota(jnp.int32, (fresh, lanes), 1)
    token = lane
    for g in range(1, group):
        token = token - jnp.where(lane >= g * fresh, fresh, 0)
    causal = lax.broadcasted_iota(jnp.int32, (fresh, lanes), 0) <= token
    for j in range(kvh):
        s = jnp.where(causal, scores(n32[0, :, j, :].astype(jnp.bfloat16), qs[j]), FLOOR)
        m = jnp.max(s, axis=0, keepdims=True)
        w = jnp.exp2((s - m) * coef)
        peaks[half, j] = m
        sums[half, j] = jnp.sum(w, axis=0, keepdims=True)
        acc[j] = mixed(n32[1, :, j, :].astype(jnp.bfloat16), w.astype(jnp.bfloat16))

    def second_phase():
        sent(0)
        start(1, k_copy)
        start(1, v_copy)

    @pl.when(side == 1)
    def _():
        second_phase()

    def arrived(copy, i, j):
        @pl.when(i > 0)
        def _():
            copy(2 * i, j, homes[1]).wait_recv()

        copy(2 * i + 1, j, homes[1]).wait_recv()

    for j in range(kvh):
        def score_block(i, _, j=j):
            arrived(k_copy, i, j)
            s = scores(recvk[j, pl.ds(2 * i, 2)].reshape(2 * SLOTS * page, hd), qs[j])
            b = bias[pl.ds(2 * i, 2)].reshape(2 * SLOTS * page, hd).astype(jnp.float32)
            s = s + jnp.concatenate([b] * (lanes // hd), axis=1)
            m = jnp.max(s, axis=0, keepdims=True)
            w = jnp.exp2((s - m) * coef)
            peaks[i, j] = m
            sums[i, j] = jnp.sum(w, axis=0, keepdims=True)
            probs[i, j] = w.astype(jnp.bfloat16)
            return 0

        lax.fori_loop(0, half, score_block, 0)

    for j in range(kvh):
        top = peaks[half, j]
        for i in range(half):
            top = jnp.maximum(top, peaks[i, j])
        total = jnp.zeros_like(top)
        for i in range(half + 1):
            scale = jnp.exp2((peaks[i, j] - top) * coef)
            total = total + sums[i, j] * scale
            peaks[i, j] = scale
        acc[j] = acc[j] * peaks[half, j]
        sums[half, j] = total

        def value_block(i, _, j=j):
            arrived(v_copy, i, j)
            part = mixed(recvv[j, pl.ds(2 * i, 2)].reshape(2 * SLOTS * page, hd), probs[i, j])
            acc[j] = acc[j] + part * peaks[i, j]
            return 0

        lax.fori_loop(0, half, value_block, 0)

    @pl.when(side == 0)
    def _():
        second_phase()

    for j in range(kvh):
        heads = (acc[j] / sums[half, j]).T.astype(jnp.bfloat16)
        for g in range(group):
            h = j * group + g
            attn[:, h * hd:(h + 1) * hd] = heads[g * fresh:(g + 1) * fresh, :]

    def sum_copy(pos, t):
        d = chunk_at(pos)
        step = jnp.where(d > mz, 1, -1)
        slot = jnp.where(d == mz - 1, n_mp, d)
        return pltpu.make_async_remote_copy(
            src_ref=sbuf.at[pos, t], dst_ref=rbuf.at[slot, t], send_sem=rs_sem.at[pos, t],
            recv_sem=rr_sem.at[slot, t], device_id={"mp": mz + step}, device_id_type=MESH,
        )

    def arrival(slot, t, source):
        return pltpu.make_async_remote_copy(
            src_ref=sbuf.at[0, t], dst_ref=rbuf.at[slot, t], send_sem=rs_sem.at[0, t],
            recv_sem=rr_sem.at[slot, t], device_id={"mp": source}, device_id_type=MESH,
        )

    def product(pos, t):
        i = pos * tiles + t
        slot = i % held
        pltpu.make_async_copy(w_hbm.at[:, pl.ds(0, width)], wbuf.at[slot], w_sem.at[i]).wait()
        return jnp.dot(attn[...], wbuf[slot], preferred_element_type=jnp.float32)

    def project(pos, t):
        d = chunk_at(pos)
        part = product(pos, t)
        if pos == 0:
            w_copy(n_mp - 1, t).start()
        relay = ((d > mz) & (mz > 0)) | ((d < mz) & (mz < n_mp - 1))

        @pl.when(d == mz)
        def _():
            own[t] = part

        @pl.when((d != mz) & relay)
        def _():
            arrival(d, t, jnp.where(d > mz, mz - 1, mz + 1)).wait_recv()
            sbuf[pos, t] = (part + rbuf[d, t].astype(jnp.float32)).astype(jnp.bfloat16)

        @pl.when((d != mz) & jnp.logical_not(relay))
        def _():
            sbuf[pos, t] = part.astype(jnp.bfloat16)

        @pl.when(d != mz)
        def _():
            sum_copy(pos, t).start()

    for group_of in [(pos,) for pos in range(n_mp - 2)] + [(n_mp - 2, n_mp - 1)]:
        def step(t, _, group_of=group_of):
            for pos in group_of:
                project(pos, t)
            return 0

        lax.fori_loop(0, tiles, step, 0)

    for t in range(tiles):
        @pl.when(mz > 0)
        def _(t=t):
            arrival(mz, t, mz - 1).wait_recv()
            own[t] = own[t] + rbuf[mz, t].astype(jnp.float32)

        @pl.when(mz < n_mp - 1)
        def _(t=t):
            arrival(n_mp, t, mz + 1).wait_recv()
            own[t] = own[t] + rbuf[n_mp, t].astype(jnp.float32)

        out_ref[:, t * width:(t + 1) * width] = own[t].astype(out_ref.dtype)

    sent(1)
    for pos in range(n_mp):
        @pl.when(chunk_at(pos) != mz)
        def _(pos=pos):
            for t in range(tiles):
                sum_copy(pos, t).wait_send()


def on_device(
    n, n_mp, queries, new_keys, new_values, pool_keys, pool_values, prefix_len, page_table, out_weight
):
    reqs, fresh, heads, hd = queries.shape
    pages, kvh, page, _ = pool_keys.shape
    lanes = heads // kvh * fresh
    depth, model = out_weight.shape
    chunk = model // n_mp
    width = min(512, chunk)
    tiles = chunk // width
    bf16, f32 = jnp.bfloat16, jnp.float32
    dma = pltpu.SemaphoreType.DMA
    pages_shape = (kvh, n, SLOTS, page, hd)
    out = pl.pallas_call(
        functools.partial(kernel, (n, n_mp, tiles, width)),
        out_shape=pltpu.VMEM((fresh, chunk), bf16),
        in_specs=[pl.BlockSpec(memory_space=pltpu.HBM)] * 8,
        out_specs=pl.BlockSpec(memory_space=pltpu.VMEM),
        scratch_shapes=[
            pltpu.SMEM(prefix_len.shape, jnp.int32),
            pltpu.SMEM(page_table.shape, jnp.int32),
            pltpu.VMEM(new_keys.shape, bf16),
            pltpu.VMEM(new_values.shape, bf16),
            pltpu.VMEM(pool_keys.shape, bf16),
            pltpu.VMEM(pool_values.shape, bf16),
            pltpu.VMEM(queries.shape, bf16),
            pltpu.VMEM(((n_mp - 1) * tiles, depth, width), bf16),
            pltpu.VMEM((fresh, heads, hd), f32),
            pltpu.VMEM((2, fresh, kvh, hd), f32),
            pltpu.VMEM((kvh, lanes, hd), bf16),
            pltpu.VMEM((n, SLOTS * page, hd), bf16),
            pltpu.VMEM(pages_shape, bf16),
            pltpu.VMEM(pages_shape, bf16),
            pltpu.VMEM(pages_shape, bf16),
            pltpu.VMEM(pages_shape, bf16),
            pltpu.VMEM((n // 2, kvh, 2 * SLOTS * page, lanes), bf16),
            pltpu.VMEM((n // 2 + 1, kvh, 1, lanes), f32),
            pltpu.VMEM((n // 2 + 1, kvh, 1, lanes), f32),
            pltpu.VMEM((kvh, hd, lanes), f32),
            pltpu.VMEM((fresh, depth), bf16),
            pltpu.VMEM((n_mp, tiles, fresh, width), bf16),
            pltpu.VMEM((n_mp + 1, tiles, fresh, width), bf16),
            pltpu.VMEM((tiles, fresh, width), f32),
            pltpu.SMEM((n * SLOTS,), jnp.int32),
            pltpu.SMEM((n * SLOTS,), jnp.int32),
            dma((7,)),
            dma((n_mp * tiles,)),
            dma((n, kvh)), dma((n, kvh)), dma((n, kvh)), dma((n, kvh)),
            dma((n_mp, tiles)), dma((n_mp + 1, tiles)),
        ],
        compiler_params=pltpu.CompilerParams(
            collective_id=0, has_side_effects=True, vmem_limit_bytes=60 * 2**20
        ),
    )(
        prefix_len,
        page_table,
        new_keys,
        new_values,
        queries,
        pool_keys,
        pool_values,
        out_weight,
    )
    return out[None]


def solution(mesh):
    in_specs = (
        P("seq", None, "mp", None),
        P("seq", None, "mp", None),
        P("seq", None, "mp", None),
        P("seq", "mp", None, None),
        P("seq", "mp", None, None),
        P(),
        P(),
        P("mp", None),
    )
    body = functools.partial(on_device, mesh.shape["seq"], mesh.shape["mp"])
    return jax.shard_map(
        body, mesh=mesh, in_specs=in_specs, out_specs=P("seq", None, "mp"), check_vma=False
    )
```

```python
import functools
import math

import jax
import jax.numpy as jnp
from jax import lax
from jax.experimental import pallas as pl
from jax.experimental.pallas import tpu as pltpu
from jax.sharding import PartitionSpec as P

MESH = pl.DeviceIdType.MESH
SLOTS = 2
FLOOR = -1e30


def flipped(index, mask, n):
    out, bit = 0, 1
    while bit < n:
        out = out + bit * (((index // bit) + (mask // bit)) % 2)
        bit *= 2
    return out


def line_order(m, n_mp):
    ranked = sorted(range(n_mp), key=lambda d: (-abs(d - m), min(d, n_mp - 1 - d)))
    if 0 < m < n_mp - 1:
        return ranked[-1:] + ranked[:-1]
    return ranked


def kernel(
    dims, len_hbm, table_hbm, nk_hbm, nv_hbm, q_hbm, pk_hbm, pv_hbm, w_hbm, out_ref,
    len_ref, table_ref, nk_ref, nv_ref, pk_ref, pv_ref, q_ref,
    wbuf, q32, n32, qs, bias, sendk, sendv, recvk, recvv, probs, peaks, sums, acc, attn,
    sbuf, rbuf, own, ahead, ids_ref, live_ref,
    in_sem, w_sem, ks_sem, kr_sem, vs_sem, vr_sem, rs_sem, rr_sem,
):
    n, n_mp, tiles, width = dims
    half = n // 2
    held = (n_mp - 1) * tiles
    fresh = q_ref.shape[1]
    pages, kvh, page, hd = pk_ref.shape
    maxp = table_ref.shape[1]
    group = q_ref.shape[2] // kvh
    lanes = group * fresh
    me = lax.axis_index("seq")
    mz = lax.axis_index("mp")
    side = me % 2
    coef = math.log2(math.e) / math.sqrt(hd)

    loads = [
        pltpu.make_async_copy(src, dst, in_sem.at[i])
        for i, (src, dst) in enumerate((
            (len_hbm, len_ref), (table_hbm, table_ref), (pk_hbm, pk_ref), (pv_hbm, pv_ref),
            (q_hbm, q_ref), (nk_hbm, nk_ref), (nv_hbm, nv_ref),
        ))
    ]
    orders = [line_order(m, n_mp) for m in range(n_mp)]

    def chunk_at(pos):
        out = jnp.int32(orders[0][pos])
        for m in range(1, n_mp):
            out = jnp.where(mz == m, orders[m][pos], out)
        return out

    def w_copy(pos, t):
        col = pl.multiple_of((chunk_at(pos) * tiles + t) * width, 128)
        i = pos * tiles + t
        return pltpu.make_async_copy(w_hbm.at[:, pl.ds(col, width)], wbuf.at[i % held], w_sem.at[i])

    barrier = pltpu.get_barrier_semaphore()
    for k in range(1, n):
        pl.semaphore_signal(
            barrier, inc=1, device_id={"seq": flipped(me, k, n)}, device_id_type=MESH
        )

    @pl.when(mz > 0)
    def _():
        pl.semaphore_signal(barrier, inc=1, device_id={"mp": mz - 1}, device_id_type=MESH)

    @pl.when(mz < n_mp - 1)
    def _():
        pl.semaphore_signal(barrier, inc=1, device_id={"mp": mz + 1}, device_id_type=MESH)

    for load in loads:
        load.start()

    def scan(row, owner):
        first, count = owner * pages, 0
        ids = [0] * SLOTS
        live = [0] * SLOTS
        length = len_ref[row]
        for l in range(maxp):
            p = table_ref[row, l]
            owned = (p >= first) & (p < first + pages)
            room = jnp.clip(length - l * page, 0, page)
            for s in range(SLOTS):
                here = owned & (count == s)
                ids[s] = jnp.where(here, p - first, ids[s])
                live[s] = jnp.where(here, room, live[s])
            count = count + owned.astype(jnp.int32)
        return ids, live

    def find(k, _):
        other = flipped(me, k, n)
        ids, _ = scan(other, me)
        _, live = scan(me, other)
        for s in range(SLOTS):
            ids_ref[k * SLOTS + s] = ids[s]
            live_ref[k * SLOTS + s] = live[s]
        return 0

    loads[0].wait()
    loads[1].wait()
    lax.fori_loop(0, n, find, 0)

    homes = []
    for q in range(half):
        home, bit = me - side, 2
        while bit < n:
            if 2 * q & bit:
                home = home + jnp.where(lax.rem(lax.div(me, bit), 2) == 0, bit, -bit)
            bit *= 2
        homes.append(home)

    def page_copy(send, recv, s_sem, r_sem, k, j, target):
        return pltpu.make_async_remote_copy(
            src_ref=send.at[j, k], dst_ref=recv.at[j, k], send_sem=s_sem.at[k, j],
            recv_sem=r_sem.at[k, j], device_id={"seq": target}, device_id_type=MESH,
        )

    def k_copy(k, j, target):
        return page_copy(sendk, recvk, ks_sem, kr_sem, k, j, target)

    def v_copy(k, j, target):
        return page_copy(sendv, recvv, vs_sem, vr_sem, k, j, target)

    def targets(phase, act):
        off = side if phase == 0 else 1 - side
        for q in reversed(range(1, half)):
            act(2 * q + off, homes[q] + phase)

        @pl.when(side != phase)
        def _():
            act(1, homes[0] + phase)

    def pack(pool, send):
        def one(k, target):
            for s in range(SLOTS):
                for j in range(kvh):
                    send[j, k, s] = pool[ids_ref[k * SLOTS + s], j]
        return one

    def start(phase, copy):
        for j in range(kvh):
            targets(phase, lambda k, target: copy(k, j, target).start())

    def sent(phase):
        for copy in (k_copy, v_copy):
            for j in range(kvh):
                targets(phase, lambda k, target: copy(k, j, target).wait_send())

    loads[2].wait()
    targets(0, pack(pk_ref, sendk))
    around = jnp.where(mz > 0, 1, 0) + jnp.where(mz < n_mp - 1, 1, 0)
    pl.semaphore_wait(barrier, n - 1 + around)
    start(0, k_copy)
    loads[3].wait()
    targets(0, pack(pv_ref, sendv))
    start(0, v_copy)
    targets(1, pack(pk_ref, sendk))
    targets(1, pack(pv_ref, sendv))
    pack(pk_ref, recvk)(0, me)
    pack(pv_ref, recvv)(0, me)
    for i in range(4, 7):
        loads[i].wait()
    for pos in range(n_mp - 1):
        for t in range(tiles):
            w_copy(pos, t).start()

    row = lax.broadcasted_iota(jnp.int32, (SLOTS * page, hd), 0)

    def mask(k, _):
        allowed = row < live_ref[k * SLOTS]
        for i in range(1, SLOTS):
            allowed = allowed | ((row >= i * page) & (row < i * page + live_ref[k * SLOTS + i]))
        bias[k] = jnp.where(allowed, 0.0, FLOOR).astype(jnp.bfloat16)
        return 0

    lax.fori_loop(0, n, mask, 0)
    q32[...] = q_ref[0].astype(jnp.float32)
    n32[0] = nk_ref[0].astype(jnp.float32)
    n32[1] = nv_ref[0].astype(jnp.float32)
    for h in range(kvh * group):
        j, g = h // group, h % group
        qs[j, g * fresh:(g + 1) * fresh, :] = q32[:, h, :].astype(jnp.bfloat16)

    def scores(keys, queries):
        return lax.dot_general(
            keys, queries, (((1,), (1,)), ((), ())), preferred_element_type=jnp.float32
        )

    def mixed(values, weights):
        return lax.dot_general(
            values, weights, (((0,), (0,)), ((), ())), preferred_element_type=jnp.float32
        )

    lane = lax.broadcasted_iota(jnp.int32, (fresh, lanes), 1)
    token = lane
    for g in range(1, group):
        token = token - jnp.where(lane >= g * fresh, fresh, 0)
    causal = lax.broadcasted_iota(jnp.int32, (fresh, lanes), 0) <= token
    for j in range(kvh):
        s = jnp.where(causal, scores(n32[0, :, j, :].astype(jnp.bfloat16), qs[j]), FLOOR)
        m = jnp.max(s, axis=0, keepdims=True)
        w = jnp.exp2((s - m) * coef)
        peaks[half, j] = m
        sums[half, j] = jnp.sum(w, axis=0, keepdims=True)
        acc[j] = mixed(n32[1, :, j, :].astype(jnp.bfloat16), w.astype(jnp.bfloat16))

    split = (kvh - 1) * group * hd

    def w_wait(i):
        pltpu.make_async_copy(w_hbm.at[:, pl.ds(0, width)], wbuf.at[i % held], w_sem.at[i]).wait()

    def second_phase():
        sent(0)
        start(1, k_copy)
        start(1, v_copy)

    @pl.when(side == 1)
    def _():
        second_phase()

    def arrived(copy, i, j):
        @pl.when(i > 0)
        def _():
            copy(2 * i, j, homes[1]).wait_recv()

        copy(2 * i + 1, j, homes[1]).wait_recv()

    for j in range(kvh):
        def score_block(i, _, j=j):
            arrived(k_copy, i, j)
            s = scores(recvk[j, pl.ds(2 * i, 2)].reshape(2 * SLOTS * page, hd), qs[j])
            b = bias[pl.ds(2 * i, 2)].reshape(2 * SLOTS * page, hd).astype(jnp.float32)
            s = s + jnp.concatenate([b] * (lanes // hd), axis=1)
            m = jnp.max(s, axis=0, keepdims=True)
            w = jnp.exp2((s - m) * coef)
            peaks[i, j] = m
            sums[i, j] = jnp.sum(w, axis=0, keepdims=True)
            probs[i, j] = w.astype(jnp.bfloat16)
            return 0

        lax.fori_loop(0, half, score_block, 0)

    for j in range(kvh):
        top = peaks[half, j]
        for i in range(half):
            top = jnp.maximum(top, peaks[i, j])
        total = jnp.zeros_like(top)
        for i in range(half + 1):
            scale = jnp.exp2((peaks[i, j] - top) * coef)
            total = total + sums[i, j] * scale
            peaks[i, j] = scale
        acc[j] = acc[j] * peaks[half, j]
        sums[half, j] = total

        def value_block(i, _, j=j):
            arrived(v_copy, i, j)
            part = mixed(recvv[j, pl.ds(2 * i, 2)].reshape(2 * SLOTS * page, hd), probs[i, j])
            acc[j] = acc[j] + part * peaks[i, j]
            return 0

        lax.fori_loop(0, half, value_block, 0)
        heads = (acc[j] * (1.0 / sums[half, j])).T.astype(jnp.bfloat16)
        for g in range(group):
            h = j * group + g
            attn[:, h * hd:(h + 1) * hd] = heads[g * fresh:(g + 1) * fresh, :]
        if j == kvh - 2:
            w_wait(0)
            ahead[...] = jnp.dot(attn[:, :split], wbuf[0, :split], preferred_element_type=jnp.float32)

    def sum_copy(pos, t):
        d = chunk_at(pos)
        step = jnp.where(d > mz, 1, -1)
        slot = jnp.where(d == mz - 1, n_mp, d)
        return pltpu.make_async_remote_copy(
            src_ref=sbuf.at[pos, t], dst_ref=rbuf.at[slot, t], send_sem=rs_sem.at[pos, t],
            recv_sem=rr_sem.at[slot, t], device_id={"mp": mz + step}, device_id_type=MESH,
        )

    def arrival(slot, t, source):
        return pltpu.make_async_remote_copy(
            src_ref=sbuf.at[0, t], dst_ref=rbuf.at[slot, t], send_sem=rs_sem.at[0, t],
            recv_sem=rr_sem.at[slot, t], device_id={"mp": source}, device_id_type=MESH,
        )

    def product(pos, t):
        i = pos * tiles + t
        slot = i % held
        if split and isinstance(t, int):
            rest = jnp.dot(attn[:, split:], wbuf[0, split:], preferred_element_type=jnp.float32)
            return ahead[...] + rest
        w_wait(i)
        return jnp.dot(attn[...], wbuf[slot], preferred_element_type=jnp.float32)

    def project(pos, t):
        d = chunk_at(pos)
        part = product(pos, t)
        if pos == 0:
            w_copy(n_mp - 1, t).start()
        relay = ((d > mz) & (mz > 0)) | ((d < mz) & (mz < n_mp - 1))

        @pl.when(d == mz)
        def _():
            own[t] = part

        @pl.when((d != mz) & relay)
        def _():
            arrival(d, t, jnp.where(d > mz, mz - 1, mz + 1)).wait_recv()
            sbuf[pos, t] = (part + rbuf[d, t].astype(jnp.float32)).astype(jnp.bfloat16)

        @pl.when((d != mz) & jnp.logical_not(relay))
        def _():
            sbuf[pos, t] = part.astype(jnp.bfloat16)

        @pl.when(d != mz)
        def _():
            sum_copy(pos, t).start()

    @pl.when(side == 0)
    def _():
        second_phase()

    project(0, 0)

    for group_of in [(pos,) for pos in range(n_mp - 2)] + [(n_mp - 2, n_mp - 1)]:
        def step(t, _, group_of=group_of):
            for pos in group_of:
                project(pos, t)
            return 0

        lax.fori_loop(0 if group_of[0] else 1, tiles, step, 0)

    for t in range(tiles):
        @pl.when(mz > 0)
        def _(t=t):
            arrival(mz, t, mz - 1).wait_recv()
            own[t] = own[t] + rbuf[mz, t].astype(jnp.float32)

        @pl.when(mz < n_mp - 1)
        def _(t=t):
            arrival(n_mp, t, mz + 1).wait_recv()
            own[t] = own[t] + rbuf[n_mp, t].astype(jnp.float32)

        out_ref[:, t * width:(t + 1) * width] = own[t].astype(out_ref.dtype)

    sent(1)
    for pos in range(n_mp):
        @pl.when(chunk_at(pos) != mz)
        def _(pos=pos):
            for t in range(tiles):
                sum_copy(pos, t).wait_send()


def on_device(
    n, n_mp, queries, new_keys, new_values, pool_keys, pool_values, prefix_len, page_table, out_weight
):
    reqs, fresh, heads, hd = queries.shape
    pages, kvh, page, _ = pool_keys.shape
    lanes = heads // kvh * fresh
    depth, model = out_weight.shape
    chunk = model // n_mp
    width = min(512, chunk)
    tiles = chunk // width
    bf16, f32 = jnp.bfloat16, jnp.float32
    dma = pltpu.SemaphoreType.DMA
    pages_shape = (kvh, n, SLOTS, page, hd)
    out = pl.pallas_call(
        functools.partial(kernel, (n, n_mp, tiles, width)),
        out_shape=pltpu.VMEM((fresh, chunk), bf16),
        in_specs=[pl.BlockSpec(memory_space=pltpu.HBM)] * 8,
        out_specs=pl.BlockSpec(memory_space=pltpu.VMEM),
        scratch_shapes=[
            pltpu.SMEM(prefix_len.shape, jnp.int32),
            pltpu.SMEM(page_table.shape, jnp.int32),
            pltpu.VMEM(new_keys.shape, bf16),
            pltpu.VMEM(new_values.shape, bf16),
            pltpu.VMEM(pool_keys.shape, bf16),
            pltpu.VMEM(pool_values.shape, bf16),
            pltpu.VMEM(queries.shape, bf16),
            pltpu.VMEM(((n_mp - 1) * tiles, depth, width), bf16),
            pltpu.VMEM((fresh, heads, hd), f32),
            pltpu.VMEM((2, fresh, kvh, hd), f32),
            pltpu.VMEM((kvh, lanes, hd), bf16),
            pltpu.VMEM((n, SLOTS * page, hd), bf16),
            pltpu.VMEM(pages_shape, bf16),
            pltpu.VMEM(pages_shape, bf16),
            pltpu.VMEM(pages_shape, bf16),
            pltpu.VMEM(pages_shape, bf16),
            pltpu.VMEM((n // 2, kvh, 2 * SLOTS * page, lanes), bf16),
            pltpu.VMEM((n // 2 + 1, kvh, 1, lanes), f32),
            pltpu.VMEM((n // 2 + 1, kvh, 1, lanes), f32),
            pltpu.VMEM((kvh, hd, lanes), f32),
            pltpu.VMEM((fresh, depth), bf16),
            pltpu.VMEM((n_mp, tiles, fresh, width), bf16),
            pltpu.VMEM((n_mp + 1, tiles, fresh, width), bf16),
            pltpu.VMEM((tiles, fresh, width), f32),
            pltpu.VMEM((fresh, width), f32),
            pltpu.SMEM((n * SLOTS,), jnp.int32),
            pltpu.SMEM((n * SLOTS,), jnp.int32),
            dma((7,)),
            dma((n_mp * tiles,)),
            dma((n, kvh)), dma((n, kvh)), dma((n, kvh)), dma((n, kvh)),
            dma((n_mp, tiles)), dma((n_mp + 1, tiles)),
        ],
        compiler_params=pltpu.CompilerParams(
            collective_id=0, has_side_effects=True, vmem_limit_bytes=60 * 2**20
        ),
    )(
        prefix_len,
        page_table,
        new_keys,
        new_values,
        queries,
        pool_keys,
        pool_values,
        out_weight,
    )
    return out[None]


def solution(mesh):
    in_specs = (
        P("seq", None, "mp", None),
        P("seq", None, "mp", None),
        P("seq", None, "mp", None),
        P("seq", "mp", None, None),
        P("seq", "mp", None, None),
        P(),
        P(),
        P("mp", None),
    )
    body = functools.partial(on_device, mesh.shape["seq"], mesh.shape["mp"])
    return jax.shard_map(
        body, mesh=mesh, in_specs=in_specs, out_specs=P("seq", None, "mp"), check_vma=False
    )
```

```python
import functools
import math

import jax
import jax.numpy as jnp
from jax import lax
from jax.experimental import pallas as pl
from jax.experimental.pallas import tpu as pltpu
from jax.sharding import PartitionSpec as P

MESH = pl.DeviceIdType.MESH
SLOTS = 2
FLOOR = -1e30


def flipped(index, mask, n):
    out, bit = 0, 1
    while bit < n:
        out = out + bit * (((index // bit) + (mask // bit)) % 2)
        bit *= 2
    return out


def line_order(m, n_mp):
    ranked = sorted(range(n_mp), key=lambda d: (-abs(d - m), min(d, n_mp - 1 - d)))
    if 0 < m < n_mp - 1:
        return ranked[-1:] + ranked[:-1]
    return ranked


def kernel(
    dims, len_hbm, table_hbm, nk_hbm, nv_hbm, q_hbm, pk_hbm, pv_hbm, w_hbm, out_ref,
    len_ref, table_ref, nk_ref, nv_ref, pk_ref, pv_ref, q_ref,
    wbuf, q32, n32, qs, bias, sendk, sendv, recvk, recvv, probs, peaks, sums, acc, attn,
    sbuf, rbuf, own, ahead, ids_ref, live_ref,
    in_sem, w_sem, ks_sem, kr_sem, vs_sem, vr_sem, rs_sem, rr_sem,
):
    n, n_mp, tiles, width = dims
    half = n // 2
    held = (n_mp - 1) * tiles
    fresh = q_ref.shape[1]
    pages, kvh, page, hd = pk_ref.shape
    maxp = table_ref.shape[1]
    group = q_ref.shape[2] // kvh
    lanes = group * fresh
    me = lax.axis_index("seq")
    mz = lax.axis_index("mp")
    side = me % 2
    coef = math.log2(math.e) / math.sqrt(hd)

    loads = [
        pltpu.make_async_copy(src, dst, in_sem.at[i])
        for i, (src, dst) in enumerate((
            (len_hbm, len_ref), (table_hbm, table_ref), (pk_hbm, pk_ref), (pv_hbm, pv_ref),
            (q_hbm, q_ref), (nk_hbm, nk_ref), (nv_hbm, nv_ref),
        ))
    ]
    orders = [line_order(m, n_mp) for m in range(n_mp)]

    def chunk_at(pos):
        out = jnp.int32(orders[0][pos])
        for m in range(1, n_mp):
            out = jnp.where(mz == m, orders[m][pos], out)
        return out

    def w_copy(pos, t):
        col = pl.multiple_of((chunk_at(pos) * tiles + t) * width, 128)
        i = pos * tiles + t
        return pltpu.make_async_copy(w_hbm.at[:, pl.ds(col, width)], wbuf.at[i % held], w_sem.at[i])

    barrier = pltpu.get_barrier_semaphore()
    for k in range(1, n):
        pl.semaphore_signal(
            barrier, inc=1, device_id={"seq": flipped(me, k, n)}, device_id_type=MESH
        )

    @pl.when(mz > 0)
    def _():
        pl.semaphore_signal(barrier, inc=1, device_id={"mp": mz - 1}, device_id_type=MESH)

    @pl.when(mz < n_mp - 1)
    def _():
        pl.semaphore_signal(barrier, inc=1, device_id={"mp": mz + 1}, device_id_type=MESH)

    for load in loads:
        load.start()

    def scan(row, owner):
        first, count = owner * pages, 0
        ids = [0] * SLOTS
        live = [0] * SLOTS
        length = len_ref[row]
        for l in range(maxp):
            p = table_ref[row, l]
            owned = (p >= first) & (p < first + pages)
            room = jnp.clip(length - l * page, 0, page)
            for s in range(SLOTS):
                here = owned & (count == s)
                ids[s] = jnp.where(here, p - first, ids[s])
                live[s] = jnp.where(here, room, live[s])
            count = count + owned.astype(jnp.int32)
        return ids, live

    def find(k, _):
        other = flipped(me, k, n)
        ids, _ = scan(other, me)
        _, live = scan(me, other)
        for s in range(SLOTS):
            ids_ref[k * SLOTS + s] = ids[s]
            live_ref[k * SLOTS + s] = live[s]
        return 0

    loads[0].wait()
    loads[1].wait()
    lax.fori_loop(0, n, find, 0)

    homes = []
    for q in range(half):
        home, bit = me - side, 2
        while bit < n:
            if 2 * q & bit:
                home = home + jnp.where(lax.rem(lax.div(me, bit), 2) == 0, bit, -bit)
            bit *= 2
        homes.append(home)

    def page_copy(send, recv, s_sem, r_sem, k, j, target):
        return pltpu.make_async_remote_copy(
            src_ref=send.at[j, k], dst_ref=recv.at[j, k], send_sem=s_sem.at[k, j],
            recv_sem=r_sem.at[k, j], device_id={"seq": target}, device_id_type=MESH,
        )

    def k_copy(k, j, target):
        return page_copy(sendk, recvk, ks_sem, kr_sem, k, j, target)

    def v_copy(k, j, target):
        return page_copy(sendv, recvv, vs_sem, vr_sem, k, j, target)

    def targets(phase, act):
        off = side if phase == 0 else 1 - side
        for q in reversed(range(1, half)):
            act(2 * q + off, homes[q] + phase)

        @pl.when(side != phase)
        def _():
            act(1, homes[0] + phase)

    def pack(pool, send):
        def one(k, target):
            for s in range(SLOTS):
                for j in range(kvh):
                    send[j, k, s] = pool[ids_ref[k * SLOTS + s], j]
        return one

    def start(phase, copy):
        for j in range(kvh):
            targets(phase, lambda k, target: copy(k, j, target).start())

    def sent(phase):
        for copy in (k_copy, v_copy):
            for j in range(kvh):
                targets(phase, lambda k, target: copy(k, j, target).wait_send())

    loads[2].wait()
    targets(0, pack(pk_ref, sendk))
    around = jnp.where(mz > 0, 1, 0) + jnp.where(mz < n_mp - 1, 1, 0)
    pl.semaphore_wait(barrier, n - 1 + around)
    start(0, k_copy)
    loads[3].wait()
    targets(0, pack(pv_ref, sendv))
    start(0, v_copy)
    targets(1, pack(pk_ref, sendk))
    targets(1, pack(pv_ref, sendv))
    pack(pk_ref, recvk)(0, me)
    pack(pv_ref, recvv)(0, me)
    for i in range(4, 7):
        loads[i].wait()
    for pos in range(n_mp - 1):
        for t in range(tiles):
            w_copy(pos, t).start()

    row = lax.broadcasted_iota(jnp.int32, (SLOTS * page, hd), 0)

    def mask(k, _):
        allowed = row < live_ref[k * SLOTS]
        for i in range(1, SLOTS):
            allowed = allowed | ((row >= i * page) & (row < i * page + live_ref[k * SLOTS + i]))
        bias[k] = jnp.where(allowed, 0.0, FLOOR).astype(jnp.bfloat16)
        return 0

    lax.fori_loop(0, n, mask, 0)
    q32[...] = q_ref[0].astype(jnp.float32)
    n32[0] = nk_ref[0].astype(jnp.float32)
    n32[1] = nv_ref[0].astype(jnp.float32)
    for h in range(kvh * group):
        j, g = h // group, h % group
        qs[j, g * fresh:(g + 1) * fresh, :] = q32[:, h, :].astype(jnp.bfloat16)

    def scores(keys, queries):
        return lax.dot_general(
            keys, queries, (((1,), (1,)), ((), ())), preferred_element_type=jnp.float32
        )

    def mixed(values, weights):
        return lax.dot_general(
            values, weights, (((0,), (0,)), ((), ())), preferred_element_type=jnp.float32
        )

    lane = lax.broadcasted_iota(jnp.int32, (fresh, lanes), 1)
    token = lane
    for g in range(1, group):
        token = token - jnp.where(lane >= g * fresh, fresh, 0)
    causal = lax.broadcasted_iota(jnp.int32, (fresh, lanes), 0) <= token
    for j in range(kvh):
        s = jnp.where(causal, scores(n32[0, :, j, :].astype(jnp.bfloat16), qs[j]), FLOOR)
        m = jnp.max(s, axis=0, keepdims=True)
        w = jnp.exp2((s - m) * coef)
        peaks[half, j] = m
        sums[half, j] = jnp.sum(w, axis=0, keepdims=True)
        acc[j] = mixed(n32[1, :, j, :].astype(jnp.bfloat16), w.astype(jnp.bfloat16))

    split = (kvh - 1) * group * hd

    def w_wait(i):
        pltpu.make_async_copy(w_hbm.at[:, pl.ds(0, width)], wbuf.at[i % held], w_sem.at[i]).wait()

    def second_phase():
        start(1, k_copy)
        start(1, v_copy)

    @pl.when(side == 1)
    def _():
        sent(0)
        second_phase()

    def arrived(copy, i, j):
        @pl.when(i > 0)
        def _():
            copy(2 * i, j, homes[1]).wait_recv()

        copy(2 * i + 1, j, homes[1]).wait_recv()

    for j in range(kvh):
        def score_block(i, _, j=j):
            arrived(k_copy, i, j)
            s = scores(recvk[j, pl.ds(2 * i, 2)].reshape(2 * SLOTS * page, hd), qs[j])
            b = bias[pl.ds(2 * i, 2)].reshape(2 * SLOTS * page, hd).astype(jnp.float32)
            s = s + jnp.concatenate([b] * (lanes // hd), axis=1)
            m = jnp.max(s, axis=0, keepdims=True)
            w = jnp.exp2((s - m) * coef)
            peaks[i, j] = m
            sums[i, j] = jnp.sum(w, axis=0, keepdims=True)
            probs[i, j] = w.astype(jnp.bfloat16)
            return 0

        lax.fori_loop(0, half, score_block, 0)

    for j in range(kvh):
        top = peaks[half, j]
        for i in range(half):
            top = jnp.maximum(top, peaks[i, j])
        total = jnp.zeros_like(top)
        for i in range(half + 1):
            scale = jnp.exp2((peaks[i, j] - top) * coef)
            total = total + sums[i, j] * scale
            peaks[i, j] = scale
        acc[j] = acc[j] * peaks[half, j]
        sums[half, j] = total

        def value_block(i, _, j=j):
            arrived(v_copy, i, j)
            part = mixed(recvv[j, pl.ds(2 * i, 2)].reshape(2 * SLOTS * page, hd), probs[i, j])
            acc[j] = acc[j] + part * peaks[i, j]
            return 0

        lax.fori_loop(0, half, value_block, 0)
        heads = (acc[j] * (1.0 / sums[half, j])).T.astype(jnp.bfloat16)
        for g in range(group):
            h = j * group + g
            attn[:, h * hd:(h + 1) * hd] = heads[g * fresh:(g + 1) * fresh, :]
        if j == kvh - 2:
            w_wait(0)
            ahead[...] = jnp.dot(attn[:, :split], wbuf[0, :split], preferred_element_type=jnp.float32)

    def sum_copy(pos, t):
        d = chunk_at(pos)
        step = jnp.where(d > mz, 1, -1)
        slot = jnp.where(d == mz - 1, n_mp, d)
        return pltpu.make_async_remote_copy(
            src_ref=sbuf.at[pos, t], dst_ref=rbuf.at[slot, t], send_sem=rs_sem.at[pos, t],
            recv_sem=rr_sem.at[slot, t], device_id={"mp": mz + step}, device_id_type=MESH,
        )

    def arrival(slot, t, source):
        return pltpu.make_async_remote_copy(
            src_ref=sbuf.at[0, t], dst_ref=rbuf.at[slot, t], send_sem=rs_sem.at[0, t],
            recv_sem=rr_sem.at[slot, t], device_id={"mp": source}, device_id_type=MESH,
        )

    def product(pos, t):
        i = pos * tiles + t
        slot = i % held
        if split and isinstance(t, int):
            rest = jnp.dot(attn[:, split:], wbuf[0, split:], preferred_element_type=jnp.float32)
            return ahead[...] + rest
        w_wait(i)
        return jnp.dot(attn[...], wbuf[slot], preferred_element_type=jnp.float32)

    def project(pos, t):
        d = chunk_at(pos)
        part = product(pos, t)
        if pos == 0:
            w_copy(n_mp - 1, t).start()
        relay = ((d > mz) & (mz > 0)) | ((d < mz) & (mz < n_mp - 1))

        @pl.when(d == mz)
        def _():
            own[t] = part

        @pl.when((d != mz) & relay)
        def _():
            arrival(d, t, jnp.where(d > mz, mz - 1, mz + 1)).wait_recv()
            sbuf[pos, t] = (part + rbuf[d, t].astype(jnp.float32)).astype(jnp.bfloat16)

        @pl.when((d != mz) & jnp.logical_not(relay))
        def _():
            sbuf[pos, t] = part.astype(jnp.bfloat16)

        @pl.when(d != mz)
        def _():
            sum_copy(pos, t).start()

    @pl.when(side == 0)
    def _():
        second_phase()

    project(0, 0)

    for group_of in [(pos,) for pos in range(n_mp - 2)] + [(n_mp - 2, n_mp - 1)]:
        def step(t, _, group_of=group_of):
            for pos in group_of:
                project(pos, t)
            return 0

        lax.fori_loop(0 if group_of[0] else 1, tiles, step, 0)

    for t in range(tiles):
        @pl.when(mz > 0)
        def _(t=t):
            arrival(mz, t, mz - 1).wait_recv()
            own[t] = own[t] + rbuf[mz, t].astype(jnp.float32)

        @pl.when(mz < n_mp - 1)
        def _(t=t):
            arrival(n_mp, t, mz + 1).wait_recv()
            own[t] = own[t] + rbuf[n_mp, t].astype(jnp.float32)

        out_ref[:, t * width:(t + 1) * width] = own[t].astype(out_ref.dtype)

    @pl.when(side == 0)
    def _():
        sent(0)

    sent(1)
    for pos in range(n_mp):
        @pl.when(chunk_at(pos) != mz)
        def _(pos=pos):
            for t in range(tiles):
                sum_copy(pos, t).wait_send()


def on_device(
    n, n_mp, queries, new_keys, new_values, pool_keys, pool_values, prefix_len, page_table, out_weight
):
    reqs, fresh, heads, hd = queries.shape
    pages, kvh, page, _ = pool_keys.shape
    lanes = heads // kvh * fresh
    depth, model = out_weight.shape
    chunk = model // n_mp
    width = min(512, chunk)
    tiles = chunk // width
    bf16, f32 = jnp.bfloat16, jnp.float32
    dma = pltpu.SemaphoreType.DMA
    pages_shape = (kvh, n, SLOTS, page, hd)
    out = pl.pallas_call(
        functools.partial(kernel, (n, n_mp, tiles, width)),
        out_shape=pltpu.VMEM((fresh, chunk), bf16),
        in_specs=[pl.BlockSpec(memory_space=pltpu.HBM)] * 8,
        out_specs=pl.BlockSpec(memory_space=pltpu.VMEM),
        scratch_shapes=[
            pltpu.SMEM(prefix_len.shape, jnp.int32),
            pltpu.SMEM(page_table.shape, jnp.int32),
            pltpu.VMEM(new_keys.shape, bf16),
            pltpu.VMEM(new_values.shape, bf16),
            pltpu.VMEM(pool_keys.shape, bf16),
            pltpu.VMEM(pool_values.shape, bf16),
            pltpu.VMEM(queries.shape, bf16),
            pltpu.VMEM(((n_mp - 1) * tiles, depth, width), bf16),
            pltpu.VMEM((fresh, heads, hd), f32),
            pltpu.VMEM((2, fresh, kvh, hd), f32),
            pltpu.VMEM((kvh, lanes, hd), bf16),
            pltpu.VMEM((n, SLOTS * page, hd), bf16),
            pltpu.VMEM(pages_shape, bf16),
            pltpu.VMEM(pages_shape, bf16),
            pltpu.VMEM(pages_shape, bf16),
            pltpu.VMEM(pages_shape, bf16),
            pltpu.VMEM((n // 2, kvh, 2 * SLOTS * page, lanes), bf16),
            pltpu.VMEM((n // 2 + 1, kvh, 1, lanes), f32),
            pltpu.VMEM((n // 2 + 1, kvh, 1, lanes), f32),
            pltpu.VMEM((kvh, hd, lanes), f32),
            pltpu.VMEM((fresh, depth), bf16),
            pltpu.VMEM((n_mp, tiles, fresh, width), bf16),
            pltpu.VMEM((n_mp + 1, tiles, fresh, width), bf16),
            pltpu.VMEM((tiles, fresh, width), f32),
            pltpu.VMEM((fresh, width), f32),
            pltpu.SMEM((n * SLOTS,), jnp.int32),
            pltpu.SMEM((n * SLOTS,), jnp.int32),
            dma((7,)),
            dma((n_mp * tiles,)),
            dma((n, kvh)), dma((n, kvh)), dma((n, kvh)), dma((n, kvh)),
            dma((n_mp, tiles)), dma((n_mp + 1, tiles)),
        ],
        compiler_params=pltpu.CompilerParams(
            collective_id=0, has_side_effects=True, vmem_limit_bytes=60 * 2**20
        ),
    )(
        prefix_len,
        page_table,
        new_keys,
        new_values,
        queries,
        pool_keys,
        pool_values,
        out_weight,
    )
    return out[None]


def solution(mesh):
    in_specs = (
        P("seq", None, "mp", None),
        P("seq", None, "mp", None),
        P("seq", None, "mp", None),
        P("seq", "mp", None, None),
        P("seq", "mp", None, None),
        P(),
        P(),
        P("mp", None),
    )
    body = functools.partial(on_device, mesh.shape["seq"], mesh.shape["mp"])
    return jax.shard_map(
        body, mesh=mesh, in_specs=in_specs, out_specs=P("seq", None, "mp"), check_vma=False
    )
```
